32 devices in a mesh: dp: 8 (over y, x, core), mp: 4 (over z).
Axes of the slice: x: 2, y: 2, z: 4, core: 2. Of those that a mesh axis runs over, the one named last changes fastest.
Arguments:
- tokens: bfloat16 [2048, 3072], P('dp'), may hold values from -16 to 16
- weight: bfloat16 [3072, 3072], P(None, 'mp'), may hold values from -0.109375 to 0.109375
- norm_gain: float32 [128], replicated, may hold values from 0.1 to 1.9
- upstream: bfloat16 [2048, 3072], P('dp', 'mp'), may hold values from -0.176776695 to 0.176776695
Outputs:
- perturbation: float32 [3072, 3072], P('dp', 'mp')
- sharp_grad: float32 [3072, 3072], P('dp', 'mp')
The draws below stay inside these ranges and needn't reach their ends.
All inputs are finite; a program needn't handle non-finite values.
Results may differ from the reference program's by a relative error of at most 0.0028.
Values may be sent and summed in bfloat16 or wider, within the bound.
A program may use at most 64 MiB of HBM per device.

```python
import math
import jax
import jax.numpy as jnp
from jax import lax

FEAT = 3072
HEADS = 24
HEAD_DIM = 128
TOK_DEV = 256
TOKENS = 2048
N_DP = 8


def draw_tokens(key, part):
    key_values = jax.random.fold_in(key, 0)
    key_feature = jax.random.fold_in(key, 1)
    key_offset = jax.random.fold_in(key, 3)
    ramp = 0.5 + jnp.arange(FEAT, dtype=jnp.float32) / FEAT
    spread = jnp.exp(jax.random.uniform(key_feature, (FEAT,), jnp.float32, -1.15, 1.15))
    offset = 0.5 * jax.random.normal(key_offset, (1, FEAT), jnp.float32)
    values = jax.random.normal(key_values, (TOKENS, FEAT), jnp.float32) + offset
    return jnp.clip(values * ramp * spread, -16.0, 16.0).astype(jnp.bfloat16)


def draw_upstream(key, part):
    key_noise, key_pattern = jax.random.split(key)
    columns = HEADS * HEAD_DIM
    scale = TOKENS ** (-0.5)
    noise = jax.random.normal(key_noise, (TOKENS, columns), jnp.float32)
    amplitude = (5.0 / TOKENS) ** 0.5
    pattern = amplitude * jax.random.normal(key_pattern, (1, columns), jnp.float32)
    values = (noise + pattern) * scale
    return jnp.clip(values, -8.0 * scale, 8.0 * scale).astype(jnp.bfloat16)


def steps_of(own_key, extent, cuts, smallest, high):
    gain = 1.0
    for axis_at, parts in cuts:
        draws = jax.random.uniform(jax.random.fold_in(jax.random.fold_in(own_key, 6), axis_at), (parts,), jnp.float32, smallest / len(cuts), high / len(cuts))
        gain = gain * jnp.repeat(jnp.exp(draws), extent[axis_at] // parts).reshape((-1,) + (1,) * (len(extent) - 1 - axis_at))
    return gain


def bell_draw(own_key, dims, width, most, pieces=(), held_as=jnp.bfloat16):
    entries = jax.random.normal(own_key, dims, jnp.float32) * width
    if len(pieces) > 0:
        entries = steps_of(own_key, dims, pieces, -0.22, 0.18) * entries
    return jnp.clip(entries, min=-most, max=most).astype(held_as)


def setup_inputs(seed: int = 0) -> dict:
    keys = jax.random.split(jax.random.key(seed), 5)
    tokens = draw_tokens(jax.random.fold_in(keys[4], 71), 0)
    weight = bell_draw(keys[1], (FEAT, HEADS * HEAD_DIM), FEAT ** -0.5, 0.109375, ((1, 4),))
    norm_gain = jnp.clip(1.0 + 0.18 * jax.random.normal(keys[2], (HEAD_DIM,), jnp.float32), 0.1, 1.9)
    upstream = draw_upstream(jax.random.fold_in(keys[4], 71), 0)
    return dict(tokens=tokens, weight=weight, norm_gain=norm_gain, upstream=upstream)


radius_coef = 0.004

def head_backward(queries, upstream, norm_gain):
    count = queries.shape[0]
    grouped = queries.reshape(count, -1, HEAD_DIM)
    centred = grouped - lax.optimization_barrier(jnp.mean(grouped, axis=-1, keepdims=True))
    inverse = lax.rsqrt(lax.optimization_barrier(jnp.mean(centred * centred, axis=-1, keepdims=True)) + 1e-06)
    normed = centred * inverse
    scaled = upstream.astype(jnp.float32).reshape(count, -1, HEAD_DIM) * norm_gain
    result = (scaled - lax.optimization_barrier(jnp.mean(scaled, axis=-1, keepdims=True)) - normed * lax.optimization_barrier(jnp.mean(scaled * normed, axis=-1, keepdims=True))) * inverse
    return result.reshape(count, -1).astype(jnp.bfloat16)

def left_product(left, right):
    return lax.dot_general(left, right, (((0,), (0,)), ((), ())), preferred_element_type=jnp.float32)

def reference(tokens, weight, norm_gain, upstream):
    columns = HEADS * HEAD_DIM
    blocks = tokens.reshape(N_DP, TOK_DEV, FEAT)
    upper = upstream.reshape(N_DP, TOK_DEV, columns)

    def accumulate(carry, pair):
        block, grad_up = pair
        first = jnp.dot(block, weight, preferred_element_type=jnp.float32)
        first_grad = head_backward(first, grad_up, norm_gain)
        partial_sum = left_product(block, first_grad).astype(jnp.bfloat16)
        partial_sum = lax.optimization_barrier(partial_sum)
        return (carry + partial_sum.astype(jnp.float32), None)
    ascent, unused = lax.scan(accumulate, jnp.zeros((FEAT, columns), jnp.float32), (blocks, upper))
    total = jnp.sum(ascent * ascent)
    radius = radius_coef * math.sqrt(FEAT * columns)
    perturbation = ascent * (radius / (jnp.sqrt(total) + 1e-12))
    perturbed = (weight.astype(jnp.float32) + perturbation).astype(jnp.bfloat16)
    second = jnp.dot(tokens, perturbed, preferred_element_type=jnp.float32)
    second_grad = head_backward(second, upstream, norm_gain)
    sharp_grad = left_product(tokens, second_grad)
    return (perturbation, sharp_grad)
```

```python
import functools
import math

import jax
import jax.numpy as jnp
from jax import lax
from jax.experimental import pallas as pl
from jax.experimental.pallas import tpu as pltpu
from jax.sharding import PartitionSpec as P

radius_coef = 0.004
F32 = jnp.float32
BF16 = jnp.bfloat16
MESH = pl.DeviceIdType.MESH


def head_backward(queries, upstream, norm_gain):
    head_dim = norm_gain.shape[0]
    count = queries.shape[0]
    grouped = queries.reshape(count, -1, head_dim)
    centred = grouped - jnp.mean(grouped, axis=-1, keepdims=True)
    inverse = lax.rsqrt(jnp.mean(centred * centred, axis=-1, keepdims=True) + 1e-06)
    normed = centred * inverse
    scaled = upstream.astype(jnp.float32).reshape(count, -1, head_dim) * norm_gain
    result = (
        scaled
        - jnp.mean(scaled, axis=-1, keepdims=True)
        - normed * jnp.mean(scaled * normed, axis=-1, keepdims=True)
    ) * inverse
    return result.reshape(count, -1).astype(jnp.bfloat16)


def left_product(left, right):
    return lax.dot_general(
        left, right, (((0,), (0,)), ((), ())), preferred_element_type=jnp.float32
    )


def general_step(tokens, weight, norm_gain, upstream):
    rows_own = weight.shape[0] // lax.axis_size("dp")
    radius = radius_coef * math.sqrt(weight.shape[0] * weight.shape[1] * lax.axis_size("mp"))
    row_start = lax.axis_index("dp") * rows_own
    first = jnp.dot(tokens, weight, preferred_element_type=jnp.float32)
    first_grad = head_backward(first, upstream, norm_gain)
    rounded = left_product(tokens, first_grad).astype(jnp.bfloat16)
    rounded = lax.optimization_barrier(rounded)
    owned = lax.psum_scatter(rounded.astype(jnp.float32), "dp", scatter_dimension=0, tiled=True)
    local_total = jnp.sum(owned * owned)
    total = lax.psum(local_total, ("dp", "mp"))
    perturbation = owned * (radius / (jnp.sqrt(total) + 1e-12))
    own_weight = lax.dynamic_slice_in_dim(weight, row_start, rows_own, 0)
    own_perturbed = (own_weight.astype(jnp.float32) + perturbation).astype(jnp.bfloat16)
    second = jnp.dot(
        tokens,
        lax.all_gather(own_perturbed, "dp", axis=0, tiled=True),
        preferred_element_type=jnp.float32,
    )
    second_grad = head_backward(second, upstream, norm_gain)
    sharp_grad = lax.psum_scatter(
        left_product(tokens, second_grad), "dp", scatter_dimension=0, tiled=True
    )
    return (perturbation, sharp_grad)


def cube_kernel(
    radius, n_mp,
    tok_ref, w_ref, gain_ref, up_ref,
    pert_ref, sharp_ref,
    tok_t, query, grad, keep_x, keep_y,
    core_out, core_in, x_out, x_in, y_out, y_in,
    core_out2, core_in2, x_out2, x_in2, y_out2, y_in2,
    gathered, total_dp, total_mp,
    send_sem, recv_sem,
):
    shards, rows, n_tok = tok_t.shape
    half = rows // 2
    head_dim = gain_ref.shape[1]
    me = lax.axis_index("dp")
    z = lax.axis_index("mp")
    y, x, c = me // 4, (me // 2) % 2, me % 2
    oy, ox, oc = 1 - y, 1 - x, 1 - c

    def at(yy, xx, cc):
        return (yy * 2 + xx) * 2 + cc

    partner, x_peer, y_peer = at(y, x, oc), at(y, ox, c), at(oy, x, c)
    diagonal = at(oy, ox, c)
    dp_peers = [
        partner, x_peer, y_peer, at(y, ox, oc), at(oy, x, oc), diagonal, at(oy, ox, oc)
    ]
    mp_peers = [lax.rem(z + k, n_mp) for k in range(1, n_mp)]

    barrier = pltpu.get_barrier_semaphore()
    for peer in dp_peers:
        pl.semaphore_signal(barrier, inc=1, device_id={"dp": peer}, device_id_type=MESH)
    for peer in mp_peers:
        pl.semaphore_signal(barrier, inc=1, device_id={"mp": peer}, device_id_type=MESH)

    started = []

    def send(source, target, device):
        index = len(started)
        copy = pltpu.make_async_remote_copy(
            src_ref=source, dst_ref=target,
            send_sem=send_sem.at[index], recv_sem=recv_sem.at[index],
            device_id=device, device_id_type=MESH,
        )
        copy.start()
        started.append(copy)
        return copy

    def rows_of(shard):
        return pl.ds(pl.multiple_of(shard * rows, rows), rows)

    def backward():
        for head in range(query.shape[1] // head_dim):
            columns = pl.ds(head * head_dim, head_dim)
            values = query[:, columns]
            centred = values - jnp.mean(values, axis=-1, keepdims=True)
            inverse = lax.rsqrt(jnp.mean(centred * centred, axis=-1, keepdims=True) + 1e-06)
            normed = centred * inverse
            scaled = up_ref[:, columns].astype(F32) * gain_ref[...]
            result = (
                scaled
                - jnp.mean(scaled, axis=-1, keepdims=True)
                - normed * jnp.mean(scaled * normed, axis=-1, keepdims=True)
            ) * inverse
            grad[:, columns] = result.astype(BF16)

    def product(shard):
        return jnp.dot(tok_t[shard], grad[...], preferred_element_type=F32)

    def reduce_scatter(out_ref, c_out, c_in, xo, xi, yo, yi, rounded):
        chips = [(oy, ox), (y, ox), (oy, x), (y, x)]
        low, high = pl.ds(0, half), pl.ds(half, half)
        core_copies = []

        def to_partner(i):
            c_out[i] = product(at(*chips[i], oc)).astype(c_out.dtype)
            core_copies.append(send(c_out.at[i], c_in.at[i], {"dp": partner}))

        def chip_sum(i):
            mine = product(at(*chips[i], c))
            if rounded:
                mine = mine.astype(BF16).astype(F32)
            core_copies[i].wait_recv()
            return mine + c_in[i].astype(F32)

        to_partner(0)
        to_partner(1)
        value = chip_sum(0)
        xo[0] = value[:half].astype(BF16)
        x0 = send(xo.at[0], xi.at[0], {"dp": x_peer})
        yo[0] = value[half:].astype(BF16)
        y0 = send(yo.at[0], yi.at[0], {"dp": y_peer})
        to_partner(2)
        value = chip_sum(1)
        xo[1] = value[:half].astype(BF16)
        x1 = send(xo.at[1], xi.at[1], {"dp": x_peer})
        keep_x[...] = value[half:]
        to_partner(3)
        value = chip_sum(2)
        yo[1] = value[half:].astype(BF16)
        y1 = send(yo.at[1], yi.at[1], {"dp": y_peer})
        keep_y[...] = value[:half]
        out_ref[...] = chip_sum(3)
        y0.wait_recv()
        xo[2] = (keep_x[...] + yi[0].astype(F32)).astype(BF16)
        x2 = send(xo.at[2], xi.at[2], {"dp": x_peer})
        x0.wait_recv()
        yo[2] = (keep_y[...] + xi[0].astype(F32)).astype(BF16)
        y2 = send(yo.at[2], yi.at[2], {"dp": y_peer})
        x1.wait_recv()
        y1.wait_recv()
        out_ref[low] += xi[1].astype(F32)
        out_ref[high] += yi[1].astype(F32)
        x2.wait_recv()
        y2.wait_recv()
        out_ref[low] += yi[2].astype(F32)
        out_ref[high] += xi[2].astype(F32)

    for shard in range(shards):
        columns = pl.ds(shard * rows, rows)
        part = jnp.dot(tok_ref[:, columns], w_ref[columns, :], preferred_element_type=F32)
        if shard == 0:
            query[...] = part
        else:
            query[...] += part
        tok_t[shard] = tok_ref[:, columns].T
    backward()
    pl.semaphore_wait(barrier, len(dp_peers) + len(mp_peers))

    reduce_scatter(pert_ref, core_out, core_in, x_out, x_in, y_out, y_in, True)

    squares = pert_ref[...]
    squares = squares * squares
    squares = jnp.sum(squares.reshape(rows // 8, 8, squares.shape[1]), axis=0)
    folded = squares[:, :128]
    for tile in range(1, squares.shape[1] // 128):
        folded = folded + squares[:, tile * 128:(tile + 1) * 128]
    total_dp[me] = folded
    dp_copies = [send(total_dp.at[me], total_dp.at[me], {"dp": peer}) for peer in dp_peers]

    gathered[me] = pert_ref[...].astype(BF16)

    def piece(shard, which):
        return gathered.at[shard, pl.ds(which * half, half)]

    def pass_on(shard, which, device):
        return send(piece(shard, which), piece(shard, which), {"dp": device})

    ax0 = pass_on(me, 0, x_peer)
    ay0 = pass_on(me, 1, y_peer)
    own = send(gathered.at[me], gathered.at[me], {"dp": partner})
    ax1 = pass_on(me, 1, x_peer)
    ay1 = pass_on(me, 0, y_peer)

    for copy in dp_copies:
        copy.wait_recv()
    folded = total_dp[0]
    for shard in range(1, shards):
        folded = folded + total_dp[shard]
    total_mp[z] = folded
    mp_copies = [send(total_mp.at[z], total_mp.at[z], {"mp": peer}) for peer in mp_peers]

    ax0.wait_recv()
    ay2 = pass_on(x_peer, 0, y_peer)
    fwd = [pass_on(x_peer, 0, partner)]
    ay0.wait_recv()
    ax2 = pass_on(y_peer, 1, x_peer)
    fwd.append(pass_on(y_peer, 1, partner))

    for copy in mp_copies:
        copy.wait_recv()
    folded = total_mp[0]
    for index in range(1, n_mp):
        folded = folded + total_mp[index]
    scale = radius / (jnp.sqrt(jnp.sum(folded, keepdims=True)) + 1e-12)

    def second_part(shard, begin=False):
        index = rows_of(shard)
        moved = w_ref[index, :].astype(F32) + gathered[shard].astype(F32) * scale
        part = jnp.dot(tok_ref[:, index], moved.astype(BF16), preferred_element_type=F32)
        if begin:
            query[...] = part
        else:
            query[...] += part

    second_part(me, True)
    own.wait_recv()
    second_part(partner)
    pert_ref[...] = pert_ref[...] * scale
    ax1.wait_recv()
    fwd.append(pass_on(x_peer, 1, partner))
    ay1.wait_recv()
    fwd.append(pass_on(y_peer, 0, partner))
    second_part(x_peer)
    second_part(y_peer)
    fwd[0].wait_recv()
    fwd[2].wait_recv()
    second_part(at(y, ox, oc))
    fwd[1].wait_recv()
    fwd[3].wait_recv()
    second_part(at(oy, x, oc))
    ax2.wait_recv()
    fwd.append(pass_on(diagonal, 1, partner))
    ay2.wait_recv()
    fwd.append(pass_on(diagonal, 0, partner))
    second_part(diagonal)
    fwd[4].wait_recv()
    fwd[5].wait_recv()
    second_part(at(oy, ox, oc))

    backward()
    reduce_scatter(sharp_ref, core_out2, core_in2, x_out2, x_in2, y_out2, y_in2, False)
    for copy in started:
        copy.wait_send()


def cube_step(n_dp, n_mp, tokens, weight, norm_gain, upstream):
    n_tok, feat = tokens.shape
    columns = weight.shape[1]
    rows = feat // n_dp
    half = rows // 2
    radius = radius_coef * math.sqrt(feat * columns * n_mp)
    copies = 2 * 10 + 13 + (n_dp - 1) + (n_mp - 1)

    def exchange(core_type):
        return [
            pltpu.VMEM((4, rows, columns), core_type),
            pltpu.VMEM((4, rows, columns), core_type),
        ] + [pltpu.VMEM((3, half, columns), BF16)] * 4

    vmem = pl.BlockSpec(memory_space=pltpu.VMEM)
    owned = jax.ShapeDtypeStruct((rows, columns), F32)
    return pl.pallas_call(
        functools.partial(cube_kernel, radius, n_mp),
        out_shape=(owned, owned),
        in_specs=[vmem] * 4,
        out_specs=(vmem, vmem),
        scratch_shapes=[
            pltpu.VMEM((n_dp, rows, n_tok), BF16),
            pltpu.VMEM((n_tok, columns), F32),
            pltpu.VMEM((n_tok, columns), BF16),
            pltpu.VMEM((half, columns), F32),
            pltpu.VMEM((half, columns), F32),
        ]
        + exchange(BF16)
        + exchange(F32)
        + [
            pltpu.VMEM((n_dp, rows, columns), BF16),
            pltpu.VMEM((n_dp, 8, 128), F32),
            pltpu.VMEM((n_mp, 8, 128), F32),
            pltpu.SemaphoreType.DMA((copies,)),
            pltpu.SemaphoreType.DMA((copies,)),
        ],
        compiler_params=pltpu.CompilerParams(
            collective_id=0, has_side_effects=True, vmem_limit_bytes=60 * 1024 * 1024
        ),
        name="cube_step",
    )(tokens, weight, norm_gain.reshape(1, -1), upstream)


def solution(mesh):
    n_dp, n_mp = mesh.shape["dp"], mesh.shape["mp"]
    step = functools.partial(cube_step, n_dp, n_mp) if n_dp == 8 else general_step
    in_specs = (P("dp", None), P(None, "mp"), P(), P("dp", "mp"))
    out_specs = (P("dp", "mp"), P("dp", "mp"))
    return jax.shard_map(
        step, mesh=mesh, in_specs=in_specs, out_specs=out_specs, check_vma=False
    )
```

```python
import functools
import math

import jax
import jax.numpy as jnp
from jax import lax
from jax.experimental import pallas as pl
from jax.experimental.pallas import tpu as pltpu
from jax.sharding import PartitionSpec as P

radius_coef = 0.004
F32 = jnp.float32
BF16 = jnp.bfloat16
MESH = pl.DeviceIdType.MESH


def head_backward(queries, upstream, norm_gain):
    head_dim = norm_gain.shape[0]
    count = queries.shape[0]
    grouped = queries.reshape(count, -1, head_dim)
    centred = grouped - jnp.mean(grouped, axis=-1, keepdims=True)
    inverse = lax.rsqrt(jnp.mean(centred * centred, axis=-1, keepdims=True) + 1e-06)
    normed = centred * inverse
    scaled = upstream.astype(jnp.float32).reshape(count, -1, head_dim) * norm_gain
    result = (
        scaled
        - jnp.mean(scaled, axis=-1, keepdims=True)
        - normed * jnp.mean(scaled * normed, axis=-1, keepdims=True)
    ) * inverse
    return result.reshape(count, -1).astype(jnp.bfloat16)


def left_product(left, right):
    return lax.dot_general(
        left, right, (((0,), (0,)), ((), ())), preferred_element_type=jnp.float32
    )


def general_step(tokens, weight, norm_gain, upstream):
    rows_own = weight.shape[0] // lax.axis_size("dp")
    radius = radius_coef * math.sqrt(weight.shape[0] * weight.shape[1] * lax.axis_size("mp"))
    row_start = lax.axis_index("dp") * rows_own
    first = jnp.dot(tokens, weight, preferred_element_type=jnp.float32)
    first_grad = head_backward(first, upstream, norm_gain)
    rounded = left_product(tokens, first_grad).astype(jnp.bfloat16)
    rounded = lax.optimization_barrier(rounded)
    owned = lax.psum_scatter(rounded.astype(jnp.float32), "dp", scatter_dimension=0, tiled=True)
    local_total = jnp.sum(owned * owned)
    total = lax.psum(local_total, ("dp", "mp"))
    perturbation = owned * (radius / (jnp.sqrt(total) + 1e-12))
    own_weight = lax.dynamic_slice_in_dim(weight, row_start, rows_own, 0)
    own_perturbed = (own_weight.astype(jnp.float32) + perturbation).astype(jnp.bfloat16)
    second = jnp.dot(
        tokens,
        lax.all_gather(own_perturbed, "dp", axis=0, tiled=True),
        preferred_element_type=jnp.float32,
    )
    second_grad = head_backward(second, upstream, norm_gain)
    sharp_grad = lax.psum_scatter(
        left_product(tokens, second_grad), "dp", scatter_dimension=0, tiled=True
    )
    return (perturbation, sharp_grad)


def cube_kernel(
    radius, n_mp,
    tok_ref, w_hbm, gain_ref, up_ref,
    pert_ref, sharp_ref,
    weight, query, moved, delta, keep_x, keep_y,
    tok_own, tok_t, grads, grads2,
    core_out, core_in, x_out, x_in, y_out, y_in,
    total_dp, total_mp,
    load_sem, send_sem, recv_sem,
):
    shards, n_tok, rows = tok_own.shape
    half = n_tok // 2
    head_dim = gain_ref.shape[1]
    me = lax.axis_index("dp")
    z = lax.axis_index("mp")
    y, x, c = me // 4, (me // 2) % 2, me % 2
    oy, ox, oc = 1 - y, 1 - x, 1 - c

    loads = []
    for shard in range(shards):
        part = pl.ds(shard * rows, rows)
        loads.append(
            pltpu.make_async_copy(w_hbm.at[part], weight.at[part], load_sem.at[shard])
        )
        loads[-1].start()

    def at(yy, xx, cc):
        return (yy * 2 + xx) * 2 + cc

    partner, x_peer, y_peer = at(y, x, oc), at(y, ox, c), at(oy, x, c)
    x_cross, y_cross = at(y, ox, oc), at(oy, x, oc)
    diagonal, far = at(oy, ox, c), at(oy, ox, oc)
    remote = [x_peer, y_peer, x_cross, y_cross, diagonal, far]
    dp_peers = [partner] + remote
    mp_peers = [lax.rem(z + k, n_mp) for k in range(1, n_mp)]
    parity = z % 2
    z_pair = z + 1 - 2 * parity

    barrier = pltpu.get_barrier_semaphore()
    for peer in dp_peers:
        pl.semaphore_signal(barrier, inc=1, device_id={"dp": peer}, device_id_type=MESH)
    for peer in mp_peers:
        pl.semaphore_signal(barrier, inc=1, device_id={"mp": peer}, device_id_type=MESH)

    started = []

    def send(source, target, device):
        index = len(started)
        copy = pltpu.make_async_remote_copy(
            src_ref=source, dst_ref=target,
            send_sem=send_sem.at[index], recv_sem=recv_sem.at[index],
            device_id=device, device_id_type=MESH,
        )
        copy.start()
        started.append(copy)
        return copy

    def columns_of(shard):
        return pl.ds(pl.multiple_of(shard * rows, rows), rows)

    def backward(out, low):
        span = pl.ds(low, half)
        for head in range(query.shape[1] // head_dim):
            columns = pl.ds(head * head_dim, head_dim)
            values = query[span, columns]
            centred = values - jnp.mean(values, axis=-1, keepdims=True)
            inverse = lax.rsqrt(jnp.mean(centred * centred, axis=-1, keepdims=True) + 1e-06)
            normed = centred * inverse
            scaled = up_ref[span, columns].astype(F32) * gain_ref[...]
            result = (
                scaled
                - jnp.mean(scaled, axis=-1, keepdims=True)
                - normed * jnp.mean(scaled * normed, axis=-1, keepdims=True)
            ) * inverse
            out[me, span, columns] = result.astype(BF16)

    def gather(buffer, ready, consume):
        def pass_on(shard, which, device):
            block = buffer.at[shard, pl.ds(which * half, half)]
            return send(block, block, {"dp": device})

        backward(buffer, 0)
        x0 = pass_on(me, 0, x_peer)
        backward(buffer, half)
        y0 = pass_on(me, 1, y_peer)
        x1 = pass_on(me, 1, x_peer)
        y1 = pass_on(me, 0, y_peer)
        own = send(buffer.at[me], buffer.at[me], {"dp": partner})
        ready()
        consume(me)
        x0.wait_recv()
        y2 = pass_on(x_peer, 0, y_peer)
        y0.wait_recv()
        x2 = pass_on(y_peer, 1, x_peer)
        f0 = pass_on(x_peer, 0, partner)
        f1 = pass_on(y_peer, 1, partner)
        own.wait_recv()
        consume(partner)
        x1.wait_recv()
        f2 = pass_on(x_peer, 1, partner)
        y1.wait_recv()
        f3 = pass_on(y_peer, 0, partner)
        consume(x_peer)
        consume(y_peer)
        f0.wait_recv()
        f2.wait_recv()
        consume(x_cross)
        f1.wait_recv()
        f3.wait_recv()
        consume(y_cross)
        x2.wait_recv()
        f4 = pass_on(diagonal, 1, partner)
        y2.wait_recv()
        f5 = pass_on(diagonal, 0, partner)
        consume(diagonal)
        f4.wait_recv()
        f5.wait_recv()
        consume(far)

    def product(shard):
        return jnp.dot(tok_own[shard], moved[...], preferred_element_type=F32)

    def reduce_scatter(between):
        chips = [(oy, ox), (y, ox), (oy, x), (y, x)]
        low, high = pl.ds(0, half), pl.ds(half, half)
        core_copies = []

        def to_partner(i):
            core_out[i] = product(at(*chips[i], oc)).astype(BF16)
            core_copies.append(send(core_out.at[i], core_in.at[i], {"dp": partner}))

        def chip_sum(i):
            mine = product(at(*chips[i], c))
            core_copies[i].wait_recv()
            return mine + core_in[i].astype(F32)

        to_partner(0)
        to_partner(1)
        value = chip_sum(0)
        x_out[0] = value[:half].astype(BF16)
        x0 = send(x_out.at[0], x_in.at[0], {"dp": x_peer})
        y_out[0] = value[half:].astype(BF16)
        y0 = send(y_out.at[0], y_in.at[0], {"dp": y_peer})
        to_partner(2)
        value = chip_sum(1)
        x_out[1] = value[:half].astype(BF16)
        x1 = send(x_out.at[1], x_in.at[1], {"dp": x_peer})
        keep_x[...] = value[half:]
        to_partner(3)
        value = chip_sum(2)
        y_out[1] = value[half:].astype(BF16)
        y1 = send(y_out.at[1], y_in.at[1], {"dp": y_peer})
        keep_y[...] = value[:half]
        between()
        y0.wait_recv()
        x_out[2] = (keep_x[...] + y_in[0].astype(F32)).astype(BF16)
        x2 = send(x_out.at[2], x_in.at[2], {"dp": x_peer})
        x0.wait_recv()
        y_out[2] = (keep_y[...] + x_in[0].astype(F32)).astype(BF16)
        y2 = send(y_out.at[2], y_in.at[2], {"dp": y_peer})
        delta[...] = chip_sum(3)
        x1.wait_recv()
        y1.wait_recv()
        delta[low] += x_in[1].astype(F32)
        delta[high] += y_in[1].astype(F32)
        y2.wait_recv()
        delta[low] += y_in[2].astype(F32)
        x2.wait_recv()
        delta[high] += x_in[2].astype(F32)

    pl.semaphore_wait(barrier, len(dp_peers) + len(mp_peers))
    share = pl.ds(pl.multiple_of(parity * half, half), half)
    brought = [
        send(tok_ref.at[share, columns_of(peer)], tok_own.at[me, share], {"dp": peer})
        for peer in remote
    ]
    from_partner = send(
        tok_ref.at[:, columns_of(partner)], tok_own.at[me], {"dp": partner}
    )
    passed = []

    def pass_pair(index):
        brought[index].wait_recv()
        block = tok_own.at[remote[index], share]
        passed.append(send(block, block, {"mp": z_pair}))

    for shard in range(shards):
        columns = pl.ds(shard * rows, rows)
        loads[shard].wait()
        part = jnp.dot(tok_ref[:, columns], weight[columns, :], preferred_element_type=F32)
        if shard == 0:
            query[...] = part
        else:
            query[...] += part
    tok_own[me] = tok_ref[:, columns_of(me)]
    for index in range(4):
        pass_pair(index)

    def add_ascent(shard):
        if shard is not me:
            if shard is partner:
                from_partner.wait_recv()
            else:
                for index, peer in enumerate(remote):
                    if peer is shard:
                        passed[index].wait_recv()
        turned = tok_own[shard].T
        tok_t[shard] = turned
        part = jnp.dot(turned, grads[shard], preferred_element_type=F32)
        part = part.astype(BF16).astype(F32)
        if shard is me:
            pert_ref[...] = part
        else:
            pert_ref[...] += part

    def pass_rest():
        for index in range(4, 6):
            pass_pair(index)

    gather(grads, pass_rest, add_ascent)

    squares = pert_ref[...]
    moved[...] = squares.astype(BF16)
    squares = squares * squares
    squares = jnp.sum(squares.reshape(rows // 8, 8, squares.shape[1]), axis=0)
    folded = squares[:, :128]
    for tile in range(1, squares.shape[1] // 128):
        folded = folded + squares[:, tile * 128:(tile + 1) * 128]
    total_dp[me] = folded
    dp_copies = [send(total_dp.at[me], total_dp.at[me], {"dp": peer}) for peer in dp_peers]
    mp_copies = []

    def over_planes():
        for copy in dp_copies:
            copy.wait_recv()
        summed = total_dp[0]
        for shard in range(1, shards):
            summed = summed + total_dp[shard]
        total_mp[z] = summed
        for peer in mp_peers:
            mp_copies.append(send(total_mp.at[z], total_mp.at[z], {"mp": peer}))

    reduce_scatter(over_planes)
    for copy in mp_copies:
        copy.wait_recv()
    summed = total_mp[0]
    for index in range(1, n_mp):
        summed = summed + total_mp[index]
    scale = radius / (jnp.sqrt(jnp.sum(summed, keepdims=True)) + 1e-12)

    query[...] += delta[...] * scale

    def write_perturbation():
        pert_ref[...] = pert_ref[...] * scale

    def add_sharp(shard):
        part = jnp.dot(tok_t[shard], grads2[shard], preferred_element_type=F32)
        if shard is me:
            sharp_ref[...] = part
        else:
            sharp_ref[...] += part

    gather(grads2, write_perturbation, add_sharp)
    for copy in started:
        copy.wait_send()


def cube_step(n_dp, n_mp, tokens, weight, norm_gain, upstream):
    n_tok, feat = tokens.shape
    columns = weight.shape[1]
    rows = feat // n_dp
    half = n_tok // 2
    radius = radius_coef * math.sqrt(feat * columns * n_mp)
    copies = 13 + 2 * 13 + 10 + (n_dp - 1) + (n_mp - 1)
    vmem = pl.BlockSpec(memory_space=pltpu.VMEM)
    owned = jax.ShapeDtypeStruct((rows, columns), F32)
    return pl.pallas_call(
        functools.partial(cube_kernel, radius, n_mp),
        out_shape=(owned, owned),
        in_specs=[vmem, pl.BlockSpec(memory_space=pl.ANY), vmem, vmem],
        out_specs=(vmem, vmem),
        scratch_shapes=[
            pltpu.VMEM((feat, columns), BF16),
            pltpu.VMEM((n_tok, columns), F32),
            pltpu.VMEM((rows, columns), BF16),
            pltpu.VMEM((n_tok, columns), F32),
            pltpu.VMEM((half, columns), F32),
            pltpu.VMEM((half, columns), F32),
            pltpu.VMEM((n_dp, n_tok, rows), BF16),
            pltpu.VMEM((n_dp, rows, n_tok), BF16),
            pltpu.VMEM((n_dp, n_tok, columns), BF16),
            pltpu.VMEM((n_dp, n_tok, columns), BF16),
            pltpu.VMEM((4, n_tok, columns), BF16),
            pltpu.VMEM((4, n_tok, columns), BF16),
        ]
        + [pltpu.VMEM((3, half, columns), BF16)] * 4
        + [
            pltpu.VMEM((n_dp, 8, 128), F32),
            pltpu.VMEM((n_mp, 8, 128), F32),
            pltpu.SemaphoreType.DMA((n_dp,)),
            pltpu.SemaphoreType.DMA((copies,)),
            pltpu.SemaphoreType.DMA((copies,)),
        ],
        compiler_params=pltpu.CompilerParams(
            collective_id=0, has_side_effects=True, vmem_limit_bytes=60 * 1024 * 1024
        ),
        name="cube_step",
    )(tokens, weight, norm_gain.reshape(1, -1), upstream)


def solution(mesh):
    n_dp, n_mp = mesh.shape["dp"], mesh.shape["mp"]
    step = functools.partial(cube_step, n_dp, n_mp) if n_dp == 8 and n_mp % 2 == 0 else general_step
    in_specs = (P("dp", None), P(None, "mp"), P(), P("dp", "mp"))
    out_specs = (P("dp", "mp"), P("dp", "mp"))
    return jax.shard_map(
        step, mesh=mesh, in_specs=in_specs, out_specs=out_specs, check_vma=False
    )
```

```python
import functools
import math

import jax
import jax.numpy as jnp
from jax import lax
from jax.experimental import pallas as pl
from jax.experimental.pallas import tpu as pltpu
from jax.sharding import PartitionSpec as P

radius_coef = 0.004
F32 = jnp.float32
BF16 = jnp.bfloat16
MESH = pl.DeviceIdType.MESH


def head_backward(queries, upstream, norm_gain):
    head_dim = norm_gain.shape[0]
    count = queries.shape[0]
    grouped = queries.reshape(count, -1, head_dim)
    centred = grouped - jnp.mean(grouped, axis=-1, keepdims=True)
    inverse = lax.rsqrt(jnp.mean(centred * centred, axis=-1, keepdims=True) + 1e-06)
    normed = centred * inverse
    scaled = upstream.astype(jnp.float32).reshape(count, -1, head_dim) * norm_gain
    result = (
        scaled
        - jnp.mean(scaled, axis=-1, keepdims=True)
        - normed * jnp.mean(scaled * normed, axis=-1, keepdims=True)
    ) * inverse
    return result.reshape(count, -1).astype(jnp.bfloat16)


def left_product(left, right):
    return lax.dot_general(
        left, right, (((0,), (0,)), ((), ())), preferred_element_type=jnp.float32
    )


def general_step(tokens, weight, norm_gain, upstream):
    rows_own = weight.shape[0] // lax.axis_size("dp")
    radius = radius_coef * math.sqrt(weight.shape[0] * weight.shape[1] * lax.axis_size("mp"))
    row_start = lax.axis_index("dp") * rows_own
    first = jnp.dot(tokens, weight, preferred_element_type=jnp.float32)
    first_grad = head_backward(first, upstream, norm_gain)
    rounded = left_product(tokens, first_grad).astype(jnp.bfloat16)
    rounded = lax.optimization_barrier(rounded)
    owned = lax.psum_scatter(rounded.astype(jnp.float32), "dp", scatter_dimension=0, tiled=True)
    local_total = jnp.sum(owned * owned)
    total = lax.psum(local_total, ("dp", "mp"))
    perturbation = owned * (radius / (jnp.sqrt(total) + 1e-12))
    own_weight = lax.dynamic_slice_in_dim(weight, row_start, rows_own, 0)
    own_perturbed = (own_weight.astype(jnp.float32) + perturbation).astype(jnp.bfloat16)
    second = jnp.dot(
        tokens,
        lax.all_gather(own_perturbed, "dp", axis=0, tiled=True),
        preferred_element_type=jnp.float32,
    )
    second_grad = head_backward(second, upstream, norm_gain)
    sharp_grad = lax.psum_scatter(
        left_product(tokens, second_grad), "dp", scatter_dimension=0, tiled=True
    )
    return (perturbation, sharp_grad)


def cube_kernel(
    radius, n_mp,
    tok_ref, w_hbm, gain_ref, up_ref,
    pert_ref, sharp_ref,
    weight, query, moved, delta, keep_x, keep_y,
    tok_own, tok_t, grads, grads2,
    core_out, core_in, x_out, x_in, y_out, y_in,
    total_dp, total_mp,
    load_sem, send_sem, recv_sem,
):
    shards, n_tok, rows = tok_own.shape
    half = n_tok // 2
    width = query.shape[1] // 2
    head_dim = gain_ref.shape[1]
    me = lax.axis_index("dp")
    z = lax.axis_index("mp")
    y, x, c = me // 4, (me // 2) % 2, me % 2
    oy, ox, oc = 1 - y, 1 - x, 1 - c

    loads = []
    for shard in range(shards):
        part = pl.ds(shard * rows, rows)
        loads.append(
            pltpu.make_async_copy(w_hbm.at[part], weight.at[part], load_sem.at[shard])
        )
        loads[-1].start()

    def at(yy, xx, cc):
        return (yy * 2 + xx) * 2 + cc

    partner, x_peer, y_peer = at(y, x, oc), at(y, ox, c), at(oy, x, c)
    x_cross, y_cross = at(y, ox, oc), at(oy, x, oc)
    diagonal, far = at(oy, ox, c), at(oy, ox, oc)
    remote = [x_peer, y_peer, x_cross, y_cross, diagonal, far]
    dp_peers = [partner] + remote
    mp_peers = [lax.rem(z + k, n_mp) for k in range(1, n_mp)]
    parity = z % 2
    z_pair = z + 1 - 2 * parity

    barrier = pltpu.get_barrier_semaphore()
    for peer in dp_peers:
        pl.semaphore_signal(barrier, inc=1, device_id={"dp": peer}, device_id_type=MESH)
    for peer in mp_peers:
        pl.semaphore_signal(barrier, inc=1, device_id={"mp": peer}, device_id_type=MESH)

    started = []

    def send(source, target, device):
        index = len(started)
        copy = pltpu.make_async_remote_copy(
            src_ref=source, dst_ref=target,
            send_sem=send_sem.at[index], recv_sem=recv_sem.at[index],
            device_id=device, device_id_type=MESH,
        )
        copy.start()
        started.append(copy)
        return copy

    def columns_of(shard):
        return pl.ds(pl.multiple_of(shard * rows, rows), rows)

    def backward(out, part, low):
        span = pl.ds(low, half)
        for head in range(width // head_dim):
            columns = pl.ds(part * width + head * head_dim, head_dim)
            values = query[span, columns]
            centred = values - jnp.mean(values, axis=-1, keepdims=True)
            inverse = lax.rsqrt(jnp.mean(centred * centred, axis=-1, keepdims=True) + 1e-06)
            normed = centred * inverse
            scaled = up_ref[span, columns].astype(F32) * gain_ref[...]
            result = (
                scaled
                - jnp.mean(scaled, axis=-1, keepdims=True)
                - normed * jnp.mean(scaled * normed, axis=-1, keepdims=True)
            ) * inverse
            out[part, me, span, pl.ds(head * head_dim, head_dim)] = result.astype(BF16)

    def gather(buffer, part, consume):
        def pass_on(shard, which, device):
            block = buffer.at[part, shard, pl.ds(which * half, half)]
            return send(block, block, {"dp": device})

        backward(buffer, part, 0)
        x0 = pass_on(me, 0, x_peer)
        backward(buffer, part, half)
        y0 = pass_on(me, 1, y_peer)
        own = send(buffer.at[part, me], buffer.at[part, me], {"dp": partner})
        yield
        x1 = pass_on(me, 1, x_peer)
        y1 = pass_on(me, 0, y_peer)
        yield
        consume(part, me)
        yield
        x0.wait_recv()
        y2 = pass_on(x_peer, 0, y_peer)
        y0.wait_recv()
        x2 = pass_on(y_peer, 1, x_peer)
        f0 = pass_on(x_peer, 0, partner)
        f1 = pass_on(y_peer, 1, partner)
        yield
        own.wait_recv()
        consume(part, partner)
        yield
        x1.wait_recv()
        f2 = pass_on(x_peer, 1, partner)
        y1.wait_recv()
        f3 = pass_on(y_peer, 0, partner)
        consume(part, x_peer)
        consume(part, y_peer)
        yield
        f0.wait_recv()
        f2.wait_recv()
        consume(part, x_cross)
        f1.wait_recv()
        f3.wait_recv()
        consume(part, y_cross)
        yield
        x2.wait_recv()
        f4 = pass_on(diagonal, 1, partner)
        y2.wait_recv()
        f5 = pass_on(diagonal, 0, partner)
        consume(part, diagonal)
        yield
        f4.wait_recv()
        f5.wait_recv()
        consume(part, far)
        yield

    def product(part, shard):
        return jnp.dot(tok_own[shard], moved[part], preferred_element_type=F32)

    def reduce_scatter(part):
        chips = [(oy, ox), (y, ox), (oy, x), (y, x)]
        low, high = pl.ds(0, half), pl.ds(half, half)
        core_copies = []

        def to_partner(i):
            core_out[part, i] = product(part, at(*chips[i], oc)).astype(BF16)
            core_copies.append(
                send(core_out.at[part, i], core_in.at[part, i], {"dp": partner})
            )

        def chip_sum(i):
            mine = product(part, at(*chips[i], c))
            core_copies[i].wait_recv()
            return mine + core_in[part, i].astype(F32)

        def by_x(i):
            return send(x_out.at[part, i], x_in.at[part, i], {"dp": x_peer})

        def by_y(i):
            return send(y_out.at[part, i], y_in.at[part, i], {"dp": y_peer})

        to_partner(0)
        to_partner(1)
        yield
        value = chip_sum(0)
        x_out[part, 0] = value[:half].astype(BF16)
        x0 = by_x(0)
        y_out[part, 0] = value[half:].astype(BF16)
        y0 = by_y(0)
        to_partner(2)
        yield
        value = chip_sum(1)
        x_out[part, 1] = value[:half].astype(BF16)
        x1 = by_x(1)
        keep_x[part] = value[half:]
        to_partner(3)
        yield
        value = chip_sum(2)
        y_out[part, 1] = value[half:].astype(BF16)
        y1 = by_y(1)
        keep_y[part] = value[:half]
        yield
        y0.wait_recv()
        x_out[part, 2] = (keep_x[part] + y_in[part, 0].astype(F32)).astype(BF16)
        x2 = by_x(2)
        x0.wait_recv()
        y_out[part, 2] = (keep_y[part] + x_in[part, 0].astype(F32)).astype(BF16)
        y2 = by_y(2)
        delta[part] = chip_sum(3)
        yield
        x1.wait_recv()
        y1.wait_recv()
        delta[part, low] += x_in[part, 1].astype(F32)
        delta[part, high] += y_in[part, 1].astype(F32)
        yield
        y2.wait_recv()
        delta[part, low] += y_in[part, 2].astype(F32)
        x2.wait_recv()
        delta[part, high] += x_in[part, 2].astype(F32)
        yield

    def run(phase, steps=1):
        for _ in range(steps):
            next(phase)

    pl.semaphore_wait(barrier, len(dp_peers) + len(mp_peers))
    share = pl.ds(pl.multiple_of(parity * half, half), half)
    brought = [
        send(tok_ref.at[share, columns_of(peer)], tok_own.at[me, share], {"dp": peer})
        for peer in remote
    ]
    from_partner = send(
        tok_ref.at[:, columns_of(partner)], tok_own.at[me], {"dp": partner}
    )
    passed = []

    def pass_pair(index):
        brought[index].wait_recv()
        block = tok_own.at[remote[index], share]
        passed.append(send(block, block, {"mp": z_pair}))

    for shard in range(shards):
        columns = pl.ds(shard * rows, rows)
        loads[shard].wait()
        part = jnp.dot(tok_ref[:, columns], weight[columns, :], preferred_element_type=F32)
        if shard == 0:
            query[...] = part
        else:
            query[...] += part
    tok_own[me] = tok_ref[:, columns_of(me)]
    for index in range(4):
        pass_pair(index)

    def columns_in(part):
        return pl.ds(part * width, width)

    def add_ascent(part, shard):
        if part == 0:
            if shard is partner:
                from_partner.wait_recv()
            for index, peer in enumerate(remote):
                if peer is shard:
                    passed[index].wait_recv()
            turned = tok_own[shard].T
            tok_t[shard] = turned
        else:
            turned = tok_t[shard]
        value = jnp.dot(turned, grads[part, shard], preferred_element_type=F32)
        value = value.astype(BF16).astype(F32)
        if shard is me:
            pert_ref[:, columns_in(part)] = value
        else:
            pert_ref[:, columns_in(part)] += value

    def add_sharp(part, shard):
        value = jnp.dot(tok_t[shard], grads2[part, shard], preferred_element_type=F32)
        if shard is me:
            sharp_ref[:, columns_in(part)] = value
        else:
            sharp_ref[:, columns_in(part)] += value

    def moved_of(part):
        moved[part] = pert_ref[:, columns_in(part)].astype(BF16)

    g_a, g_b = gather(grads, 0, add_ascent), gather(grads, 1, add_ascent)
    run(g_a, 2)
    run(g_b)
    for index in range(4, 6):
        pass_pair(index)
    run(g_a, 2)
    run(g_b)
    run(g_a)
    run(g_b, 2)
    run(g_a, 2)
    run(g_b)
    run(g_a, 2)
    moved_of(0)
    r_a, r_b = reduce_scatter(0), reduce_scatter(1)
    run(r_a)
    run(g_b, 2)
    run(r_a, 2)
    run(g_b, 2)

    squares = pert_ref[...]
    squares = squares * squares
    squares = jnp.sum(squares.reshape(rows // 8, 8, squares.shape[1]), axis=0)
    folded = squares[:, :128]
    for tile in range(1, squares.shape[1] // 128):
        folded = folded + squares[:, tile * 128:(tile + 1) * 128]
    total_dp[me] = folded
    dp_copies = [send(total_dp.at[me], total_dp.at[me], {"dp": peer}) for peer in dp_peers]
    moved_of(1)
    run(r_b)
    run(r_a, 2)
    run(r_b, 2)
    for copy in dp_copies:
        copy.wait_recv()
    summed = total_dp[0]
    for shard in range(1, shards):
        summed = summed + total_dp[shard]
    total_mp[z] = summed
    mp_copies = [send(total_mp.at[z], total_mp.at[z], {"mp": peer}) for peer in mp_peers]
    run(r_a)
    run(r_b)
    run(r_a)
    run(r_b)
    for copy in mp_copies:
        copy.wait_recv()
    summed = total_mp[0]
    for index in range(1, n_mp):
        summed = summed + total_mp[index]
    scale = radius / (jnp.sqrt(jnp.sum(summed, keepdims=True)) + 1e-12)

    g_a, g_b = gather(grads2, 0, add_sharp), gather(grads2, 1, add_sharp)
    query[:, columns_in(0)] += delta[0] * scale
    run(g_a, 2)
    run(r_b, 2)
    query[:, columns_in(1)] += delta[1] * scale
    run(g_b)
    run(g_a, 2)
    run(g_b)
    run(g_a)
    pert_ref[...] = pert_ref[...] * scale
    run(g_b, 2)
    run(g_a, 2)
    run(g_b)
    run(g_a, 2)
    run(g_b, 4)
    for copy in started:
        copy.wait_send()


def cube_step(n_dp, n_mp, tokens, weight, norm_gain, upstream):
    n_tok, feat = tokens.shape
    columns = weight.shape[1]
    rows = feat // n_dp
    half = n_tok // 2
    radius = radius_coef * math.sqrt(feat * columns * n_mp)
    width = columns // 2
    copies = 13 + 4 * 13 + 2 * 10 + (n_dp - 1) + (n_mp - 1)
    vmem = pl.BlockSpec(memory_space=pltpu.VMEM)
    owned = jax.ShapeDtypeStruct((rows, columns), F32)
    return pl.pallas_call(
        functools.partial(cube_kernel, radius, n_mp),
        out_shape=(owned, owned),
        in_specs=[vmem, pl.BlockSpec(memory_space=pl.ANY), vmem, vmem],
        out_specs=(vmem, vmem),
        scratch_shapes=[
            pltpu.VMEM((feat, columns), BF16),
            pltpu.VMEM((n_tok, columns), F32),
            pltpu.VMEM((2, rows, width), BF16),
            pltpu.VMEM((2, n_tok, width), F32),
            pltpu.VMEM((2, half, width), F32),
            pltpu.VMEM((2, half, width), F32),
            pltpu.VMEM((n_dp, n_tok, rows), BF16),
            pltpu.VMEM((n_dp, rows, n_tok), BF16),
            pltpu.VMEM((2, n_dp, n_tok, width), BF16),
            pltpu.VMEM((2, n_dp, n_tok, width), BF16),
            pltpu.VMEM((2, 4, n_tok, width), BF16),
            pltpu.VMEM((2, 4, n_tok, width), BF16),
        ]
        + [pltpu.VMEM((2, 3, half, width), BF16)] * 4
        + [
            pltpu.VMEM((n_dp, 8, 128), F32),
            pltpu.VMEM((n_mp, 8, 128), F32),
            pltpu.SemaphoreType.DMA((n_dp,)),
            pltpu.SemaphoreType.DMA((copies,)),
            pltpu.SemaphoreType.DMA((copies,)),
        ],
        compiler_params=pltpu.CompilerParams(
            collective_id=0, has_side_effects=True, vmem_limit_bytes=60 * 1024 * 1024
        ),
        name="cube_step",
    )(tokens, weight, norm_gain.reshape(1, -1), upstream)


def solution(mesh):
    n_dp, n_mp = mesh.shape["dp"], mesh.shape["mp"]
    step = functools.partial(cube_step, n_dp, n_mp) if n_dp == 8 and n_mp % 2 == 0 else general_step
    in_specs = (P("dp", None), P(None, "mp"), P(), P("dp", "mp"))
    out_specs = (P("dp", "mp"), P("dp", "mp"))
    return jax.shard_map(
        step, mesh=mesh, in_specs=in_specs, out_specs=out_specs, check_vma=False
    )
```

```python
import functools
import math

import jax
import jax.numpy as jnp
from jax import lax
from jax.experimental import pallas as pl
from jax.experimental.pallas import tpu as pltpu
from jax.sharding import PartitionSpec as P

radius_coef = 0.004
F32 = jnp.float32
BF16 = jnp.bfloat16
MESH = pl.DeviceIdType.MESH


def head_backward(queries, upstream, norm_gain):
    head_dim = norm_gain.shape[0]
    count = queries.shape[0]
    grouped = queries.reshape(count, -1, head_dim)
    centred = grouped - jnp.mean(grouped, axis=-1, keepdims=True)
    inverse = lax.rsqrt(jnp.mean(centred * centred, axis=-1, keepdims=True) + 1e-06)
    normed = centred * inverse
    scaled = upstream.astype(jnp.float32).reshape(count, -1, head_dim) * norm_gain
    result = (
        scaled
        - jnp.mean(scaled, axis=-1, keepdims=True)
        - normed * jnp.mean(scaled * normed, axis=-1, keepdims=True)
    ) * inverse
    return result.reshape(count, -1).astype(jnp.bfloat16)


def left_product(left, right):
    return lax.dot_general(
        left, right, (((0,), (0,)), ((), ())), preferred_element_type=jnp.float32
    )


def general_step(tokens, weight, norm_gain, upstream):
    rows_own = weight.shape[0] // lax.axis_size("dp")
    radius = radius_coef * math.sqrt(weight.shape[0] * weight.shape[1] * lax.axis_size("mp"))
    row_start = lax.axis_index("dp") * rows_own
    first = jnp.dot(tokens, weight, preferred_element_type=jnp.float32)
    first_grad = head_backward(first, upstream, norm_gain)
    rounded = left_product(tokens, first_grad).astype(jnp.bfloat16)
    rounded = lax.optimization_barrier(rounded)
    owned = lax.psum_scatter(rounded.astype(jnp.float32), "dp", scatter_dimension=0, tiled=True)
    local_total = jnp.sum(owned * owned)
    total = lax.psum(local_total, ("dp", "mp"))
    perturbation = owned * (radius / (jnp.sqrt(total) + 1e-12))
    own_weight = lax.dynamic_slice_in_dim(weight, row_start, rows_own, 0)
    own_perturbed = (own_weight.astype(jnp.float32) + perturbation).astype(jnp.bfloat16)
    second = jnp.dot(
        tokens,
        lax.all_gather(own_perturbed, "dp", axis=0, tiled=True),
        preferred_element_type=jnp.float32,
    )
    second_grad = head_backward(second, upstream, norm_gain)
    sharp_grad = lax.psum_scatter(
        left_product(tokens, second_grad), "dp", scatter_dimension=0, tiled=True
    )
    return (perturbation, sharp_grad)


def cube_kernel(
    radius, n_mp,
    tok_ref, w_hbm, gain_ref, up_ref,
    pert_ref, sharp_ref,
    weight, query, moved, delta, keep_x, keep_y,
    tok_own, tok_t, grads, grads2,
    core_out, core_in, x_out, x_in, y_out, y_in,
    total_dp, total_mp,
    load_sem, send_sem, recv_sem,
):
    shards, n_tok, rows = tok_own.shape
    half = n_tok // 2
    width = query.shape[1] // 2
    head_dim = gain_ref.shape[1]
    me = lax.axis_index("dp")
    z = lax.axis_index("mp")
    y, x, c = me // 4, (me // 2) % 2, me % 2
    oy, ox, oc = 1 - y, 1 - x, 1 - c

    loads = []
    for shard in range(shards):
        part = pl.ds(shard * rows, rows)
        loads.append(
            pltpu.make_async_copy(w_hbm.at[part], weight.at[part], load_sem.at[shard])
        )
        loads[-1].start()

    def at(yy, xx, cc):
        return (yy * 2 + xx) * 2 + cc

    partner, x_peer, y_peer = at(y, x, oc), at(y, ox, c), at(oy, x, c)
    x_cross, y_cross = at(y, ox, oc), at(oy, x, oc)
    diagonal, far = at(oy, ox, c), at(oy, ox, oc)
    remote = [x_peer, y_peer, x_cross, y_cross, diagonal, far]
    dp_peers = [partner] + remote
    mp_peers = [lax.rem(z + k, n_mp) for k in range(1, n_mp)]
    parity = z % 2
    z_pair = z + 1 - 2 * parity

    barrier = pltpu.get_barrier_semaphore()
    for peer in dp_peers:
        pl.semaphore_signal(barrier, inc=1, device_id={"dp": peer}, device_id_type=MESH)
    for peer in mp_peers:
        pl.semaphore_signal(barrier, inc=1, device_id={"mp": peer}, device_id_type=MESH)

    started = []

    def send(source, target, device):
        index = len(started)
        copy = pltpu.make_async_remote_copy(
            src_ref=source, dst_ref=target,
            send_sem=send_sem.at[index], recv_sem=recv_sem.at[index],
            device_id=device, device_id_type=MESH,
        )
        copy.start()
        started.append(copy)
        return copy

    def columns_of(shard):
        return pl.ds(pl.multiple_of(shard * rows, rows), rows)

    def backward(out, part, low):
        span = pl.ds(low, half)
        for head in range(width // head_dim):
            columns = pl.ds(part * width + head * head_dim, head_dim)
            values = query[span, columns]
            centred = values - jnp.mean(values, axis=-1, keepdims=True)
            inverse = lax.rsqrt(jnp.mean(centred * centred, axis=-1, keepdims=True) + 1e-06)
            normed = centred * inverse
            scaled = up_ref[span, columns].astype(F32) * gain_ref[...]
            result = (
                scaled
                - jnp.mean(scaled, axis=-1, keepdims=True)
                - normed * jnp.mean(scaled * normed, axis=-1, keepdims=True)
            ) * inverse
            out[part, me, span, pl.ds(head * head_dim, head_dim)] = result.astype(BF16)

    def gather(buffer, part, consume):
        def pass_on(shard, which, device):
            block = buffer.at[part, shard, pl.ds(which * half, half)]
            return send(block, block, {"dp": device})

        backward(buffer, part, 0)
        x0 = pass_on(me, 0, x_peer)
        backward(buffer, part, half)
        y0 = pass_on(me, 1, y_peer)
        own = send(buffer.at[part, me], buffer.at[part, me], {"dp": partner})
        yield
        x1 = pass_on(me, 1, x_peer)
        y1 = pass_on(me, 0, y_peer)
        yield
        consume(part, me)
        yield
        x0.wait_recv()
        y2 = pass_on(x_peer, 0, y_peer)
        y0.wait_recv()
        x2 = pass_on(y_peer, 1, x_peer)
        f0 = pass_on(x_peer, 0, partner)
        f1 = pass_on(y_peer, 1, partner)
        yield
        own.wait_recv()
        consume(part, partner)
        yield
        x1.wait_recv()
        f2 = pass_on(x_peer, 1, partner)
        y1.wait_recv()
        f3 = pass_on(y_peer, 0, partner)
        consume(part, x_peer)
        consume(part, y_peer)
        yield
        f0.wait_recv()
        f2.wait_recv()
        consume(part, x_cross)
        f1.wait_recv()
        f3.wait_recv()
        consume(part, y_cross)
        yield
        x2.wait_recv()
        f4 = pass_on(diagonal, 1, partner)
        y2.wait_recv()
        f5 = pass_on(diagonal, 0, partner)
        consume(part, diagonal)
        yield
        f4.wait_recv()
        f5.wait_recv()
        consume(part, far)
        yield

    def product(part, shard):
        return jnp.dot(tok_own[shard], moved[part], preferred_element_type=F32)

    def reduce_scatter(part):
        chips = [(oy, ox), (y, ox), (oy, x), (y, x)]
        low, high = pl.ds(0, half), pl.ds(half, half)
        core_copies = []

        def to_partner(i):
            core_out[part, i] = product(part, at(*chips[i], oc)).astype(BF16)
            core_copies.append(
                send(core_out.at[part, i], core_in.at[part, i], {"dp": partner})
            )

        def chip_sum(i):
            mine = product(part, at(*chips[i], c))
            core_copies[i].wait_recv()
            return mine + core_in[part, i].astype(F32)

        def by_x(i):
            return send(x_out.at[part, i], x_in.at[part, i], {"dp": x_peer})

        def by_y(i):
            return send(y_out.at[part, i], y_in.at[part, i], {"dp": y_peer})

        to_partner(0)
        to_partner(1)
        yield
        value = chip_sum(0)
        x_out[part, 0] = value[:half].astype(BF16)
        x0 = by_x(0)
        y_out[part, 0] = value[half:].astype(BF16)
        y0 = by_y(0)
        to_partner(2)
        yield
        value = chip_sum(1)
        x_out[part, 1] = value[:half].astype(BF16)
        x1 = by_x(1)
        keep_x[part] = value[half:]
        to_partner(3)
        yield
        value = chip_sum(2)
        y_out[part, 1] = value[half:].astype(BF16)
        y1 = by_y(1)
        keep_y[part] = value[:half]
        yield
        y0.wait_recv()
        x_out[part, 2] = (keep_x[part] + y_in[part, 0].astype(F32)).astype(BF16)
        x2 = by_x(2)
        x0.wait_recv()
        y_out[part, 2] = (keep_y[part] + x_in[part, 0].astype(F32)).astype(BF16)
        y2 = by_y(2)
        delta[part] = chip_sum(3)
        yield
        x1.wait_recv()
        y1.wait_recv()
        delta[part, low] += x_in[part, 1].astype(F32)
        delta[part, high] += y_in[part, 1].astype(F32)
        yield
        y2.wait_recv()
        delta[part, low] += y_in[part, 2].astype(F32)
        x2.wait_recv()
        delta[part, high] += x_in[part, 2].astype(F32)
        yield

    def run(phase, steps=1):
        for _ in range(steps):
            next(phase)

    pl.semaphore_wait(barrier, len(dp_peers) + len(mp_peers))
    share = pl.ds(pl.multiple_of(parity * half, half), half)
    brought = [
        send(tok_ref.at[share, columns_of(peer)], tok_own.at[me, share], {"dp": peer})
        for peer in remote
    ]
    from_partner = send(
        tok_ref.at[:, columns_of(partner)], tok_own.at[me], {"dp": partner}
    )
    passed = []

    def pass_pair(index):
        brought[index].wait_recv()
        block = tok_own.at[remote[index], share]
        passed.append(send(block, block, {"mp": z_pair}))

    for shard in range(shards):
        columns = pl.ds(shard * rows, rows)
        loads[shard].wait()
        part = jnp.dot(tok_ref[:, columns], weight[columns, :], preferred_element_type=F32)
        if shard == 0:
            query[...] = part
        else:
            query[...] += part
    tok_own[me] = tok_ref[:, columns_of(me)]
    for index in range(4):
        pass_pair(index)

    def columns_in(part):
        return pl.ds(part * width, width)

    def add_ascent(part, shard):
        if part == 0:
            if shard is partner:
                from_partner.wait_recv()
            for index, peer in enumerate(remote):
                if peer is shard:
                    passed[index].wait_recv()
            turned = tok_own[shard].T
            tok_t[shard] = turned
        else:
            turned = tok_t[shard]
        value = jnp.dot(turned, grads[part, shard], preferred_element_type=F32)
        value = value.astype(BF16).astype(F32)
        if shard is me:
            pert_ref[:, columns_in(part)] = value
        else:
            pert_ref[:, columns_in(part)] += value

    def add_sharp(part, shard):
        value = jnp.dot(tok_t[shard], grads2[part, shard], preferred_element_type=F32)
        if shard is me:
            sharp_ref[:, columns_in(part)] = value
        else:
            sharp_ref[:, columns_in(part)] += value

    def moved_of(part):
        moved[part] = pert_ref[:, columns_in(part)].astype(BF16)

    g_a, g_b = gather(grads, 0, add_ascent), gather(grads, 1, add_ascent)
    run(g_a, 2)
    run(g_b)
    for index in range(4, 6):
        pass_pair(index)
    run(g_a, 2)
    run(g_b)
    run(g_a)
    run(g_b, 2)
    run(g_a, 2)
    run(g_b)
    run(g_a, 2)
    moved_of(0)
    r_a, r_b = reduce_scatter(0), reduce_scatter(1)
    run(r_a)
    run(g_b, 2)
    run(r_a, 2)
    run(g_b, 2)

    squares = pert_ref[...]
    squares = squares * squares
    squares = jnp.sum(squares.reshape(rows // 8, 8, squares.shape[1]), axis=0)
    folded = squares[:, :128]
    for tile in range(1, squares.shape[1] // 128):
        folded = folded + squares[:, tile * 128:(tile + 1) * 128]
    total_dp[me] = folded
    dp_copies = [send(total_dp.at[me], total_dp.at[me], {"dp": peer}) for peer in dp_peers]
    moved_of(1)
    run(r_b)
    run(r_a, 2)
    run(r_b, 2)
    for copy in dp_copies:
        copy.wait_recv()
    summed = total_dp[0]
    for shard in range(1, shards):
        summed = summed + total_dp[shard]
    total_mp[z] = summed
    mp_copies = [send(total_mp.at[z], total_mp.at[z], {"mp": peer}) for peer in mp_peers]
    run(r_a)
    run(r_b)
    run(r_a)
    run(r_b)
    for copy in mp_copies:
        copy.wait_recv()
    summed = total_mp[0]
    for index in range(1, n_mp):
        summed = summed + total_mp[index]
    scale = radius / (jnp.sqrt(jnp.sum(summed, keepdims=True)) + 1e-12)

    g_a, g_b = gather(grads2, 0, add_sharp), gather(grads2, 1, add_sharp)
    query[:, columns_in(0)] += delta[0] * scale
    run(g_a, 2)
    run(r_b, 2)
    query[:, columns_in(1)] += delta[1] * scale
    run(g_b)
    run(g_a, 2)
    run(g_b)
    run(g_a)
    pert_ref[...] = pert_ref[...] * scale
    run(g_b, 2)
    run(g_a, 2)
    run(g_b)
    run(g_a, 2)
    run(g_b, 4)
    for copy in started:
        copy.wait_send()


def cube_step(n_dp, n_mp, tokens, weight, norm_gain, upstream):
    n_tok, feat = tokens.shape
    columns = weight.shape[1]
    rows = feat // n_dp
    half = n_tok // 2
    radius = radius_coef * math.sqrt(feat * columns * n_mp)
    width = columns // 2
    copies = 13 + 4 * 13 + 2 * 10 + (n_dp - 1) + (n_mp - 1)
    vmem = pl.BlockSpec(memory_space=pltpu.VMEM)
    owned = pltpu.VMEM((rows, columns), F32)
    return pl.pallas_call(
        functools.partial(cube_kernel, radius, n_mp),
        out_shape=(owned, owned),
        in_specs=[vmem, pl.BlockSpec(memory_space=pl.ANY), vmem, vmem],
        out_specs=(vmem, vmem),
        scratch_shapes=[
            pltpu.VMEM((feat, columns), BF16),
            pltpu.VMEM((n_tok, columns), F32),
            pltpu.VMEM((2, rows, width), BF16),
            pltpu.VMEM((2, n_tok, width), F32),
            pltpu.VMEM((2, half, width), F32),
            pltpu.VMEM((2, half, width), F32),
            pltpu.VMEM((n_dp, n_tok, rows), BF16),
            pltpu.VMEM((n_dp, rows, n_tok), BF16),
            pltpu.VMEM((2, n_dp, n_tok, width), BF16),
            pltpu.VMEM((2, n_dp, n_tok, width), BF16),
            pltpu.VMEM((2, 4, n_tok, width), BF16),
            pltpu.VMEM((2, 4, n_tok, width), BF16),
        ]
        + [pltpu.VMEM((2, 3, half, width), BF16)] * 4
        + [
            pltpu.VMEM((n_dp, 8, 128), F32),
            pltpu.VMEM((n_mp, 8, 128), F32),
            pltpu.SemaphoreType.DMA((n_dp,)),
            pltpu.SemaphoreType.DMA((copies,)),
            pltpu.SemaphoreType.DMA((copies,)),
        ],
        compiler_params=pltpu.CompilerParams(
            collective_id=0, has_side_effects=True, vmem_limit_bytes=60 * 1024 * 1024
        ),
        name="cube_step",
    )(tokens, weight, norm_gain.reshape(1, -1), upstream)


def solution(mesh):
    n_dp, n_mp = mesh.shape["dp"], mesh.shape["mp"]
    step = functools.partial(cube_step, n_dp, n_mp) if n_dp == 8 and n_mp % 2 == 0 else general_step
    in_specs = (P("dp", None), P(None, "mp"), P(), P("dp", "mp"))
    out_specs = (P("dp", "mp"), P("dp", "mp"))
    return jax.shard_map(
        step, mesh=mesh, in_specs=in_specs, out_specs=out_specs, check_vma=False
    )
```
